32 devices in a mesh: tm: 8 (over y, x, core), grp: 4 (over z).
Axes of the slice: x: 2, y: 2, z: 4, core: 2. Of those that a mesh axis runs over, the one named last changes fastest.
Arguments:
- series: float32 [131072, 512], P(('tm', 'grp')), may hold values from -6 to 6
- filter_taps: float32 [33], replicated, may hold values from -1 to 1
- sign_flips: int32 [131072], P(('tm', 'grp')), may hold values from -1 to 1, as said below
- samples: int32 [8192], replicated, may hold values from 0 to 131071, as said below
Outputs:
- sketch: float32 [8192, 512], P(('tm', 'grp'))
- r_factor: float32 [512, 512], replicated
The draws below stay inside these ranges and needn't reach their ends.
Inputs may be any that keep to these rules, and one draw needn't show every extreme that they name: `sign_flips`: each entry is -1 or +1. All distinct; the values of samples modulo 4096 take exactly 4096 distinct values, each by exactly 2 consecutive entries; entries are ordered by their value modulo 4096, then by value.
All inputs are finite; a program needn't handle non-finite values.
Results may differ from the reference program's by a relative error of at most 0.0003.
Values sent between devices are 32-bit elements; how exact they have to be, the bound alone decides.
A program may use at most 128 MiB of HBM per device.

```python
import jax
import jax.numpy as jnp
from jax import lax

W = 512
TAPS = 33
HALF_TAPS = 16
SAMPLES = 8192
ROWS_DEV = 4096
ROWS = 131072
COPIES = 2
DISTINCT = 4096
N_TM = 8
N_GRP = 4


def draw_sign_flips(key, part):
    coins = jax.random.randint(jax.random.fold_in(key, 11), (ROWS,), 0, 2, dtype=jnp.int32)
    return 2 * coins - 1


def draw_samples(key, part):
    blocks_all = ROWS // ROWS_DEV
    shuffled = jax.random.permutation(jax.random.fold_in(key, 23), ROWS_DEV)
    positions = jnp.sort(shuffled[:DISTINCT]).astype(jnp.int32)
    block_keys = jax.random.split(jax.random.fold_in(key, 37), DISTINCT)

    def choose_blocks(one_key):
        return jnp.sort(jax.random.permutation(one_key, blocks_all)[:COPIES]).astype(jnp.int32)
    owners = jax.vmap(choose_blocks)(block_keys)
    return (owners * ROWS_DEV + positions[:, None]).reshape(SAMPLES).astype(jnp.int32)


def steps_of(own_key, dims, pieces, low, high):
    def one(dim, blocks):
        heights = jax.random.uniform(jax.random.fold_in(jax.random.fold_in(own_key, 6), dim), (blocks,), jnp.float32, low / len(pieces), high / len(pieces))
        return jnp.repeat(jnp.exp(heights), dims[dim] // blocks).reshape((-1,) + (1,) * (len(dims) - dim - 1))

    gain = one(*pieces[0])
    for cut in pieces[1:]:
        gain = gain * one(*cut)
    return gain


def normal_values(own_key, shape, spread, most, pieces=(), kind=jnp.bfloat16):
    factor_of = steps_of(own_key, shape, pieces, -0.22, 0.18) if pieces else 1.0
    result = jax.random.normal(own_key, shape, jnp.float32) * spread * factor_of
    return jnp.minimum(jnp.maximum(result, -most), most).astype(kind)


def setup_inputs(seed: int = 0) -> dict:
    arg_keys = jax.random.split(jax.random.key(seed), 5)
    return {
        "series": normal_values(arg_keys[0], (ROWS, W), 1.0, 6.0, ((0, 32),), jnp.float32),
        "filter_taps": normal_values(arg_keys[1], (TAPS,), TAPS ** -0.5, 1.0, (), jnp.float32),
        "sign_flips": draw_sign_flips(jax.random.fold_in(arg_keys[4], 71), 0),
        "samples": draw_samples(jax.random.fold_in(arg_keys[4], 71), 0),
    }


def bit_count(values, width_bits):
    counted = jnp.zeros_like(values)
    for offset in range(width_bits):
        counted = counted + (values >> offset & 1)
    return counted

def hadamard(order):
    row_ids = jnp.arange(order, dtype=jnp.int32)[:, None]
    col_ids = jnp.arange(order, dtype=jnp.int32)[None, :]
    parity = bit_count(row_ids & col_ids, max(order.bit_length(), 1)) & 1
    return (1 - 2 * parity).astype(jnp.float32)

def local_transform(rows_block):
    length, columns = rows_block.shape
    levels = length.bit_length() - 1
    outer = 2 ** ((levels + 1) // 2)
    inner = length // outer
    layered = rows_block.reshape(outer, inner, columns)
    layered = jnp.einsum('ux,xvw->uvw', hadamard(outer), layered, precision=lax.Precision.HIGHEST)
    layered = jnp.einsum('vy,uyw->uvw', hadamard(inner), layered, precision=lax.Precision.HIGHEST)
    return layered.reshape(length, columns)

def reference(series, filter_taps, sign_flips, samples):
    blocks_all = N_TM * N_GRP
    row_scale = 1.0 / jnp.sqrt(jnp.float32(ROWS))
    width_bits = ROWS.bit_length()

    def step(carry, owner):
        first_row = owner * ROWS_DEV
        head_rows = lax.dynamic_slice_in_dim(series, jnp.maximum(first_row - HALF_TAPS, 0).astype(jnp.int32), HALF_TAPS, 0)
        head_rows = head_rows * (owner > 0).astype(jnp.float32)
        tail_rows = lax.dynamic_slice_in_dim(series, jnp.minimum(first_row + ROWS_DEV, ROWS - HALF_TAPS).astype(jnp.int32), HALF_TAPS, 0)
        tail_rows = tail_rows * (owner < blocks_all - 1).astype(jnp.float32)
        middle = lax.dynamic_slice_in_dim(series, first_row.astype(jnp.int32), ROWS_DEV, 0)
        window = jnp.concatenate([head_rows, middle, tail_rows], axis=0)
        filtered = filter_taps[0] * window[0:ROWS_DEV]
        for offset in range(1, TAPS):
            filtered = filtered + filter_taps[offset] * window[offset:offset + ROWS_DEV]
        flips = lax.dynamic_slice_in_dim(sign_flips, first_row.astype(jnp.int32), ROWS_DEV, 0)
        flipped = filtered * flips.astype(jnp.float32)[:, None]
        mixed = local_transform(flipped)
        local_row = samples % ROWS_DEV
        owner_block = samples // ROWS_DEV
        parity = bit_count(owner_block & owner, width_bits) & 1
        weights = (1 - 2 * parity).astype(jnp.float32) * row_scale
        picked = jnp.take(mixed, local_row, axis=0) * weights[:, None]
        return (carry + picked, None)
    start_sum = jnp.zeros((SAMPLES, W), jnp.float32)
    sketch, _ = lax.scan(step, start_sum, jnp.arange(blocks_all, dtype=jnp.int32))
    gram = lax.dot_general(sketch.astype(jnp.float32), sketch.astype(jnp.float32), (((0,), (0,)), ((), ())), precision=lax.Precision.HIGHEST, preferred_element_type=jnp.float32)
    lower = jnp.linalg.cholesky(gram / SAMPLES)
    return (sketch, lower.T)
```

```python
import functools

import jax
import jax.numpy as jnp
from jax import lax
from jax.experimental import pallas as pl
from jax.experimental.pallas import tpu as pltpu
from jax.sharding import PartitionSpec as P

F32 = jnp.float32
BF16 = jnp.bfloat16


def halves(x):
    high = x.astype(BF16)
    return high, (x - high.astype(F32)).astype(BF16)


def mix_kernel(half, tap_count, perm_ref, taps_ref, x_ref, lo_ref, hi_ref, s_ref, o_ref,
               x_high, x_low, t_high, t_low, h_ref, y_ref):
    rows = x_ref.shape[0]
    fir = t_high.shape[0]
    window = t_high.shape[1]
    order = h_ref.shape[0]
    groups = rows // order
    per_device = o_ref.shape[1]

    out_id = lax.broadcasted_iota(jnp.int32, (fir, window), 0)
    in_id = lax.broadcasted_iota(jnp.int32, (fir, window), 1)
    lag = in_id - out_id
    band = jnp.zeros((fir, window), F32)
    for k in range(tap_count):
        band = jnp.where(lag == k, taps_ref[k], band)
    t_high[...], t_low[...] = halves(band)
    parity = lax.broadcasted_iota(jnp.int32, (order, order), 0) & lax.broadcasted_iota(
        jnp.int32, (order, order), 1
    )
    for shift in (4, 2, 1):
        parity = parity ^ (parity >> shift)
    h_ref[...] = (1 - 2 * (parity & 1)).astype(F32)

    x_high[0:half, :], x_low[0:half, :] = halves(lo_ref[...])
    x_high[half + rows :, :], x_low[half + rows :, :] = halves(hi_ref[...])

    def split(i, carry):
        at = pl.multiple_of(i * order, order)
        high, low = halves(x_ref[pl.ds(at, order), :])
        to = pl.multiple_of(at + half, half)
        x_high[pl.ds(to, order), :] = high
        x_low[pl.ds(to, order), :] = low
        return carry

    lax.fori_loop(0, groups, split, 0)

    def dot(a, b):
        return jnp.dot(a, b, preferred_element_type=F32)

    def group(a, carry):
        parts = []
        for part in range(order // fir):
            at = pl.multiple_of(a * order + part * fir, fir)
            high = x_high[pl.ds(at, window), :]
            low = x_low[pl.ds(at, window), :]
            parts.append(
                dot(t_high[...], high) + (dot(t_high[...], low) + dot(t_low[...], high))
            )
        filtered = jnp.concatenate(parts, axis=0)
        signed = (h_ref[...] * s_ref[pl.ds(a, 1), :]).astype(BF16)
        high, low = halves(filtered)
        y_ref[a] = dot(signed, high) + dot(signed, low)
        return carry

    lax.fori_loop(0, groups, group, 0)

    tile = 8
    cut = order // per_device

    def butterfly(b, carry):
        at = pl.multiple_of(b * tile, tile)
        values = [y_ref[a, pl.ds(at, tile), :] for a in range(groups)]
        step = 1
        while step < groups:
            for i in range(groups):
                if not i & step:
                    u, v = values[i], values[i + step]
                    values[i], values[i + step] = u + v, u - v
            step *= 2
        part = at // per_device
        row = pl.multiple_of(at % per_device, tile)
        for a in range(groups):
            o_ref[perm_ref[a * cut + part], pl.ds(row, tile), :] = values[a]
        return carry

    lax.fori_loop(0, order // tile, butterfly, 0)


def mixed_chunk(chunk, width, devices, perm, taps, series, low_rows, high_rows, signs):
    rows = series.shape[0]
    half = low_rows.shape[0]
    order = signs.shape[1]
    fir = 128
    spec = lambda r: pl.BlockSpec((r, width), lambda i, *_: (0, chunk))
    slabs = (devices, rows // devices, width)
    return pl.pallas_call(
        functools.partial(mix_kernel, half, taps.shape[0]),
        out_shape=jax.ShapeDtypeStruct(slabs, F32),
        grid_spec=pltpu.PrefetchScalarGridSpec(
            num_scalar_prefetch=2,
            grid=(1,),
            in_specs=[spec(rows), spec(half), spec(half),
                      pl.BlockSpec(signs.shape, lambda i, *_: (0, 0))],
            out_specs=pl.BlockSpec(slabs, lambda i, *_: (0, 0, 0)),
            scratch_shapes=[
                pltpu.VMEM((rows + 2 * half, width), BF16),
                pltpu.VMEM((rows + 2 * half, width), BF16),
                pltpu.VMEM((fir, fir + 2 * half), BF16),
                pltpu.VMEM((fir, fir + 2 * half), BF16),
                pltpu.VMEM((order, order), F32),
                pltpu.VMEM((rows // order, order, width), F32),
            ],
        ),
        cost_estimate=pl.CostEstimate(
            flops=rows * width * 2000, bytes_accessed=rows * width * 8, transcendentals=0
        ),
        name="mix",
    )(perm, taps, series, low_rows, high_rows, signs)


def factor_kernel(block, scale, g_ref, r_ref, m_ref, a_ref):
    size = g_ref.shape[0]
    hi = lax.Precision.HIGHEST
    a_ref[...] = g_ref[...] * scale
    tiles_count = block // 8
    eye_row = lax.broadcasted_iota(jnp.int32, (8, block), 0)
    eye_col = lax.broadcasted_iota(jnp.int32, (8, block), 1)
    sub = lax.broadcasted_iota(jnp.int32, (8, 2 * block), 0)

    def panel(p, carry):
        at = pl.multiple_of(p * block, block)
        tiles = []
        for t in range(tiles_count):
            own = a_ref[pl.ds(pl.multiple_of(at + 8 * t, 8), 8), pl.ds(at, block)]
            unit = (eye_row + 8 * t == eye_col).astype(F32)
            tiles.append(jnp.concatenate([own, unit], axis=1))
        for k in range(block):
            home, row_at = divmod(k, 8)
            row = jnp.broadcast_to(tiles[home][row_at : row_at + 1, :], (8, 2 * block))
            pivot = jnp.broadcast_to(row[:, k : k + 1], (8, 2 * block))
            m_ref[k : k + 1, :] = (row * lax.rsqrt(pivot))[0:1, block:]
            scaled = row / pivot
            for t in range(home, tiles_count):
                column = jnp.broadcast_to(tiles[t][:, k : k + 1], (8, 2 * block))
                if t == home:
                    column = jnp.where(sub > row_at, column, 0.0)
                tiles[t] = tiles[t] - column * scaled
        rows = lax.dot_general(
            m_ref[...], a_ref[pl.ds(at, block), :], (((1,), (0,)), ((), ())),
            precision=hi, preferred_element_type=F32,
        )
        keep = lax.broadcasted_iota(jnp.int32, rows.shape, 1) >= (
            lax.broadcasted_iota(jnp.int32, rows.shape, 0) + at
        )
        rows = jnp.where(keep, rows, 0.0)
        r_ref[pl.ds(at, block), :] = rows

        @pl.when(p < size // block - 1)
        def _():
            a_ref[...] -= lax.dot_general(
                rows, rows, (((0,), (0,)), ((), ())),
                precision=hi, preferred_element_type=F32,
            )
        return carry

    lax.fori_loop(0, size // block, panel, 0)


def factor(gram, sample_count):
    size = gram.shape[0]
    block = min(128, size)
    return pl.pallas_call(
        functools.partial(factor_kernel, block, 1.0 / sample_count),
        out_shape=jax.ShapeDtypeStruct(gram.shape, F32),
        in_specs=[pl.BlockSpec(memory_space=pltpu.VMEM)],
        out_specs=pl.BlockSpec(memory_space=pltpu.VMEM),
        scratch_shapes=[pltpu.VMEM((block, block), F32), pltpu.VMEM((size, size), F32)],
        name="factor",
    )(gram)


def stage_bits(tm, grp):
    grp_bits = list(range(grp.bit_length() - 1))
    base = len(grp_bits)
    tm_bits = list(range(base, base + tm.bit_length() - 1))
    core, rest = tm_bits[:1], tm_bits[1:]
    near, far = rest[: len(rest) // 2], rest[len(rest) // 2 :]
    return core + near + far + grp_bits, core + far + near + grp_bits


def pack(value, bits):
    packed = jnp.zeros_like(value)
    for bit in bits:
        packed = packed * 2 + (value >> bit & 1)
    return packed


def swap_halo(series, half):
    axes = ("tm", "grp")
    count = lax.axis_size(axes)
    forward = [(i, i + 1) for i in range(count - 1)]
    backward = [(i + 1, i) for i in range(count - 1)]
    low = lax.ppermute(series[-half:], axes, forward)
    high = lax.ppermute(series[:half], axes, backward)
    return low, high


def bit_parity(value, bits):
    parity = jnp.zeros_like(value)
    for bit in range(bits):
        parity = parity ^ (value >> bit & 1)
    return parity


CHUNKS = 2


def on_device(series, filter_taps, sign_flips, samples):
    rows_dev, columns = series.shape
    half = (filter_taps.shape[0] - 1) // 2
    tm, grp = lax.axis_size("tm"), lax.axis_size("grp")
    devices = tm * grp
    sample_count = samples.shape[0]
    per_device = rows_dev // devices
    copies = sample_count // rows_dev
    me = lax.axis_index("tm") * grp + lax.axis_index("grp")
    even, odd = stage_bits(tm, grp)
    core = even[0]

    relative = jnp.arange(devices, dtype=jnp.int32) ^ me
    other = relative >> core & 1
    as_even = (me >> core & 1) ^ other == 0
    perm = jnp.where(as_even, pack(relative, even), pack(relative, odd))
    order = min(256, rows_dev)
    signs = sign_flips.astype(F32).reshape(rows_dev // order, order)
    low, high = swap_halo(series, half)

    slot = jnp.arange(devices, dtype=jnp.int32)
    hit = perm[None, :] == slot[:, None]
    owner = (samples // rows_dev).astype(F32).reshape(devices, per_device * copies)
    owner = lax.dot_general(hit.astype(F32), owner, (((1,), (0,)), ((), ())),
                            precision=lax.Precision.HIGHEST).astype(jnp.int32)
    owner = owner[: devices // 2].reshape(devices // 2, per_device, copies).transpose(0, 2, 1)
    low_bit = 1 - (me >> core & 1)
    width = columns // CHUNKS
    tails = []
    for chunk in range(CHUNKS):
        held = mixed_chunk(chunk, width, devices, perm, filter_taps, series, low, high, signs)
        held = held[:, None]
        for even_bit, odd_bit in zip(even, odd):
            count = held.shape[0] // 2
            pairs = []
            for d in range(devices):
                bit = odd_bit if d >> core & 1 else even_bit
                pairs.append((d, d ^ (1 << bit)))
            arrived = lax.ppermute(held[count:], ("tm", "grp"), pairs)
            mine = jnp.where(low_bit == 1, even_bit, odd_bit)
            weight = (1 - 2 * (owner[:count] >> mine & 1)).astype(F32)
            held = held[:count] + weight[..., None] * arrived
        own = owner[0]
        sign = 1 - 2 * bit_parity(own & me, devices.bit_length())
        scale = 1.0 / jnp.sqrt(F32(rows_dev * devices))
        tails.append(held[0] * (sign.astype(F32) * scale)[..., None])
    sketch = jnp.concatenate(tails, axis=-1).transpose(1, 0, 2).reshape(-1, columns)
    local_gram = lax.dot_general(
        sketch, sketch, (((0,), (0,)), ((), ())),
        precision=lax.Precision.HIGHEST, preferred_element_type=F32,
    )
    gram = lax.psum(local_gram, ("tm", "grp"))
    return sketch, factor(gram, sample_count)


def solution(mesh):
    return jax.shard_map(
        on_device,
        mesh=mesh,
        in_specs=(P(("tm", "grp"), None), P(), P(("tm", "grp")), P()),
        out_specs=(P(("tm", "grp"), None), P()),
        check_vma=False,
    )
```

```python
import functools

import jax
import jax.numpy as jnp
from jax import lax
from jax.experimental import pallas as pl
from jax.experimental.pallas import tpu as pltpu
from jax.sharding import PartitionSpec as P

F32 = jnp.float32
BF16 = jnp.bfloat16


def halves(x):
    high = x.astype(BF16)
    return high, (x - high.astype(F32)).astype(BF16)


def mix_kernel(half, tap_count, perm_ref, taps_ref, x_ref, lo_ref, hi_ref, s_ref, o_ref,
               x_high, x_low, t_high, t_low, h_ref, y_ref):
    rows = x_ref.shape[0]
    fir = t_high.shape[0]
    window = t_high.shape[1]
    order = h_ref.shape[0]
    groups = rows // order
    per_device = o_ref.shape[1]

    out_id = lax.broadcasted_iota(jnp.int32, (fir, window), 0)
    in_id = lax.broadcasted_iota(jnp.int32, (fir, window), 1)
    lag = in_id - out_id
    band = jnp.zeros((fir, window), F32)
    for k in range(tap_count):
        band = jnp.where(lag == k, taps_ref[k], band)
    t_high[...], t_low[...] = halves(band)
    parity = lax.broadcasted_iota(jnp.int32, (order, order), 0) & lax.broadcasted_iota(
        jnp.int32, (order, order), 1
    )
    for shift in (4, 2, 1):
        parity = parity ^ (parity >> shift)
    h_ref[...] = (1 - 2 * (parity & 1)).astype(F32)

    x_high[0:half, :], x_low[0:half, :] = halves(lo_ref[...])
    x_high[half + rows :, :], x_low[half + rows :, :] = halves(hi_ref[...])

    def split(i, carry):
        at = pl.multiple_of(i * order, order)
        high, low = halves(x_ref[pl.ds(at, order), :])
        to = pl.multiple_of(at + half, half)
        x_high[pl.ds(to, order), :] = high
        x_low[pl.ds(to, order), :] = low
        return carry

    lax.fori_loop(0, groups, split, 0)

    def dot(a, b):
        return jnp.dot(a, b, preferred_element_type=F32)

    def group(a, carry):
        parts = []
        for part in range(order // fir):
            at = pl.multiple_of(a * order + part * fir, fir)
            high = x_high[pl.ds(at, window), :]
            low = x_low[pl.ds(at, window), :]
            parts.append(
                dot(t_high[...], high) + (dot(t_high[...], low) + dot(t_low[...], high))
            )
        filtered = jnp.concatenate(parts, axis=0)
        signed = (h_ref[...] * s_ref[pl.ds(a, 1), :]).astype(BF16)
        high, low = halves(filtered)
        y_ref[a] = dot(signed, high) + dot(signed, low)
        return carry

    lax.fori_loop(0, groups, group, 0)

    tile = 8
    cut = order // per_device

    def butterfly(b, carry):
        at = pl.multiple_of(b * tile, tile)
        values = [y_ref[a, pl.ds(at, tile), :] for a in range(groups)]
        step = 1
        while step < groups:
            for i in range(groups):
                if not i & step:
                    u, v = values[i], values[i + step]
                    values[i], values[i + step] = u + v, u - v
            step *= 2
        part = at // per_device
        row = pl.multiple_of(at % per_device, tile)
        for a in range(groups):
            o_ref[perm_ref[a * cut + part], pl.ds(row, tile), :] = values[a]
        return carry

    lax.fori_loop(0, order // tile, butterfly, 0)


def mixed(devices, perm, taps, series, low_rows, high_rows, signs):
    rows, columns = series.shape
    half = low_rows.shape[0]
    order = signs.shape[1]
    fir = 128
    width = columns // CHUNKS
    spec = lambda r: pl.BlockSpec((r, width), lambda i, *_: (0, i))
    per_device = rows // devices
    return pl.pallas_call(
        functools.partial(mix_kernel, half, taps.shape[0]),
        out_shape=jax.ShapeDtypeStruct((devices, per_device, columns), F32),
        grid_spec=pltpu.PrefetchScalarGridSpec(
            num_scalar_prefetch=2,
            grid=(CHUNKS,),
            in_specs=[spec(rows), spec(half), spec(half),
                      pl.BlockSpec(signs.shape, lambda i, *_: (0, 0))],
            out_specs=pl.BlockSpec((devices, per_device, width), lambda i, *_: (0, 0, i)),
            scratch_shapes=[
                pltpu.VMEM((rows + 2 * half, width), BF16),
                pltpu.VMEM((rows + 2 * half, width), BF16),
                pltpu.VMEM((fir, fir + 2 * half), BF16),
                pltpu.VMEM((fir, fir + 2 * half), BF16),
                pltpu.VMEM((order, order), F32),
                pltpu.VMEM((rows // order, order, width), F32),
            ],
        ),
        name="mix",
    )(perm, taps, series, low_rows, high_rows, signs)


def factor_kernel(block, scale, g_ref, r_ref, m_ref, a_ref):
    size = a_ref.shape[0]
    hi = lax.Precision.HIGHEST
    a_ref[...] = jnp.zeros_like(a_ref)
    for q, (i, j) in enumerate(upper_blocks(size // block)):
        depth = block // 8
        part = g_ref[q * depth : (q + 1) * depth].reshape(block, block)
        a_ref[i * block : (i + 1) * block, j * block : (j + 1) * block] = part * scale
    tiles_count = block // 8
    eye_row = lax.broadcasted_iota(jnp.int32, (8, block), 0)
    eye_col = lax.broadcasted_iota(jnp.int32, (8, block), 1)
    step = 4

    def lane(value, k):
        return jnp.broadcast_to(value[:, k : k + 1], (8, block))

    def panel(p, carry):
        at = pl.multiple_of(p * block, block)
        left, right = [], []
        for t in range(tiles_count):
            left.append(a_ref[pl.ds(pl.multiple_of(at + 8 * t, 8), 8), pl.ds(at, block)])
            right.append((eye_row + 8 * t == eye_col).astype(F32))
        for k in range(0, block, step):
            home, top = divmod(k, 8)
            spread = lambda v, r: jnp.broadcast_to(v[r : r + 1, :], (8, block))
            rows_l = [spread(left[home], top + j) for j in range(step)]
            rows_r = [spread(right[home], top + j) for j in range(step)]
            corner = {(i, j): lane(rows_l[i], k + j) for i in range(step) for j in range(i, step)}
            inverse, link = [], {}
            for j in range(step):
                inverse.append(lax.rsqrt(corner[j, j]))
                for i in range(j + 1, step):
                    link[j, i] = corner[j, i] * inverse[j]
                for i in range(j + 1, step):
                    for h in range(i, step):
                        corner[i, h] = corner[i, h] - link[j, i] * link[j, h]

            def solve(values):
                done = []
                for j in range(step):
                    value = values[j]
                    for i in range(j):
                        value = value - link[i, j] * done[i]
                    done.append(value * inverse[j])
                return done

            rows_l, rows_r = solve(rows_l), solve(rows_r)
            for j in range(step):
                m_ref[k + j : k + j + 1, :] = rows_r[j][0:1, :]
            first = home if top + step < 8 else home + 1
            for t in range(first, tiles_count):
                columns = solve([lane(left[t], k + j) for j in range(step)])
                for j in range(step):
                    column = columns[j]
                    if t == home:
                        column = jnp.where(eye_row >= top + step, column, 0.0)
                    left[t] = left[t] - column * rows_l[j]
                    right[t] = right[t] - column * rows_r[j]
        rows = lax.dot_general(
            m_ref[...], a_ref[pl.ds(at, block), :], (((1,), (0,)), ((), ())),
            precision=hi, preferred_element_type=F32,
        )
        keep = lax.broadcasted_iota(jnp.int32, rows.shape, 1) >= (
            lax.broadcasted_iota(jnp.int32, rows.shape, 0) + at
        )
        rows = jnp.where(keep, rows, 0.0)
        r_ref[pl.ds(at, block), :] = rows

        @pl.when(p < size // block - 1)
        def _():
            a_ref[...] -= lax.dot_general(
                rows, rows, (((0,), (0,)), ((), ())),
                precision=hi, preferred_element_type=F32,
            )
        return carry

    lax.fori_loop(0, size // block, panel, 0)


BLOCK = 128


def upper_blocks(count):
    return [(i, j) for i in range(count) for j in range(i, count)]


def factor(packed, size, sample_count):
    return pl.pallas_call(
        functools.partial(factor_kernel, BLOCK, 1.0 / sample_count),
        out_shape=jax.ShapeDtypeStruct((size, size), F32),
        in_specs=[pl.BlockSpec(memory_space=pltpu.VMEM)],
        out_specs=pl.BlockSpec(memory_space=pltpu.VMEM),
        scratch_shapes=[pltpu.VMEM((BLOCK, BLOCK), F32), pltpu.VMEM((size, size), F32)],
        name="factor",
    )(packed)


PIECES = 4


def exchange_kernel(tm, grp, scale, held_ref, owner_ref, sk_ref, gram_ref, *scratch):
    tm_bits, grp_bits = tm.bit_length() - 1, grp.bit_length() - 1
    stages = tm_bits + grp_bits
    kept, sums, part = scratch[0], scratch[1], scratch[2]
    arrived = scratch[3 : 3 + stages]
    landed = scratch[3 + stages : 3 + 2 * stages]
    keep_sem, send_sem, recv_sem = scratch[3 + 2 * stages :]
    t, g = lax.axis_index("tm"), lax.axis_index("grp")
    core = t % 2
    devices = tm * grp
    pieces, width = kept.shape[0], kept.shape[3]
    depth = kept.shape[2]

    def across_tm(bit):
        value = (t // 2**bit) % 2
        return value, (t + (1 - 2 * value) * 2**bit, g)

    peers = [across_tm(0)]
    rest = list(range(1, tm_bits))
    near, far = rest[: len(rest) // 2], rest[len(rest) // 2 :]
    for even, odd in zip(near + far, far + near):
        (v0, p0), (v1, p1) = across_tm(even), across_tm(odd)
        mix = lambda u, v: u * (1 - core) + v * core
        peers.append((mix(v0, v1), (mix(p0[0], p1[0]), g)))
    for bit in range(grp_bits):
        value = (g // 2**bit) % 2
        peers.append((value, (t, g + (1 - 2 * value) * 2**bit)))

    barrier = pltpu.get_barrier_semaphore()
    for value, peer in peers:
        pl.semaphore_signal(barrier, inc=1, device_id=peer, device_id_type=pl.DeviceIdType.MESH)
    pl.semaphore_wait(barrier, stages)

    def remote(source, target, slot, stage):
        return pltpu.make_async_remote_copy(
            src_ref=source, dst_ref=target, send_sem=send_sem.at[slot],
            recv_sem=recv_sem.at[slot], device_id=peers[stage][1],
            device_id_type=pl.DeviceIdType.MESH,
        )

    copies, keeps = {}, []
    for c in range(pieces):
        span = pl.ds(c * depth, depth)
        copies[c, 0] = remote(held_ref.at[pl.ds(devices // 2, devices // 2), span, :],
                              arrived[0].at[c], c, 0)
        copies[c, 0].start()
        keeps.append(pltpu.make_async_copy(
            held_ref.at[pl.ds(0, devices // 2), span, :], kept.at[c], keep_sem.at[c]))
        keeps[c].start()

    def weight(c, s, k, bit):
        code = owner_ref[s, k, pl.ds(c * depth, depth), :]
        sign = (1 - 2 * ((code >> bit) & 1)).astype(F32)
        return jnp.concatenate([sign] * (width // code.shape[1]), axis=1)

    def combine(c, stage, count):
        def slab(s, carry):
            for k in range(2):
                value = weight(c, s, k, stage)
                if stage == 0:
                    sums[c, s, k] = kept[c, s] + value * arrived[0][c, s]
                else:
                    sums[c, s, k] = sums[c, s, k] + value * arrived[stage][c, s, k]
            return carry

        lax.fori_loop(0, count, slab, 0)

    order = sorted(
        ((c, i) for c in range(pieces) for i in range(stages)),
        key=lambda ci: (0 if ci[1] == 0 else 2 * ci[0] + ci[1], ci[1], ci[0]),
    )
    for c, i in order:
        if i == 0:
            keeps[c].wait()
        copies[c, i].wait_recv()
        count = devices >> (i + 1)
        combine(c, i, count)
        if i + 1 < stages:
            after = count // 2
            copies[c, i + 1] = remote(
                sums.at[c, pl.ds(after, after)], arrived[i + 1].at[c],
                (i + 1) * pieces + c, i + 1)
            copies[c, i + 1].start()
        else:
            for k in range(2):
                sk_ref[k, pl.ds(c * depth, depth), :] = (
                    sums[c, 0, k] * (weight(c, 0, k, stages) * scale))

    blocks = width // BLOCK
    rows = BLOCK // 8
    total = part.shape[0]
    sketch = sk_ref[...].reshape(2 * pieces * depth, width)
    q = 0
    for i in range(blocks):
        product = lax.dot_general(
            sketch[:, i * BLOCK : (i + 1) * BLOCK], sketch[:, i * BLOCK :],
            (((0,), (0,)), ((), ())),
            precision=lax.Precision.HIGHEST, preferred_element_type=F32)
        for j in range(blocks - i):
            part[q * rows : (q + 1) * rows] = product[:, j * BLOCK : (j + 1) * BLOCK].reshape(
                rows, 8, BLOCK)
            q += 1
    if q * rows < total:
        part[q * rows :] = jnp.zeros((total - q * rows, 8, BLOCK), F32)
    offset, size = 0, total
    base = stages * pieces
    for i in range(stages):
        size //= 2
        value = peers[i][0]
        copies[i] = remote(part.at[pl.ds(offset + (1 - value) * size, size)],
                           landed[i], base + i, i)
        copies[i].start()
        offset = offset + value * size
        copies[i].wait_recv()
        part[pl.ds(offset, size)] = part[pl.ds(offset, size)] + landed[i][...]
    gram_ref[pl.ds(offset, size)] = part[pl.ds(offset, size)]
    for i in reversed(range(stages)):
        slot = base + stages + i
        span = pl.ds(offset, size)
        back = remote(gram_ref.at[span], gram_ref.at[span], slot, i)
        back.start()
        back.wait()
        offset = offset - peers[i][0] * size
        size *= 2
    for copy in copies.values():
        copy.wait_send()


def exchange(tm, grp, scale, held, owners):
    devices, per_device, width = held.shape
    stages = (tm * grp).bit_length() - 1
    pieces = min(PIECES, per_device // 8)
    depth = per_device // pieces
    blocks = width // BLOCK
    needed = blocks * (blocks + 1) // 2 * (BLOCK // 8)
    total = -(-needed // devices) * devices
    sem = pltpu.SemaphoreType.DMA
    arrived = [pltpu.VMEM((pieces, devices // 2, depth, width), F32)] + [
        pltpu.VMEM((pieces, devices >> (i + 1), 2, depth, width), F32) for i in range(1, stages)]
    landed = [pltpu.VMEM((total >> (i + 1), 8, BLOCK), F32) for i in range(stages)]
    return pl.pallas_call(
        functools.partial(exchange_kernel, tm, grp, scale),
        out_shape=(jax.ShapeDtypeStruct((2, per_device, width), F32),
                   jax.ShapeDtypeStruct((total, 8, BLOCK), F32)),
        in_specs=[pl.BlockSpec(memory_space=pl.ANY), pl.BlockSpec(memory_space=pltpu.VMEM)],
        out_specs=(pl.BlockSpec(memory_space=pltpu.VMEM),) * 2,
        scratch_shapes=[
            pltpu.VMEM((pieces, devices // 2, depth, width), F32),
            pltpu.VMEM((pieces, devices // 2, 2, depth, width), F32),
            pltpu.VMEM((total, 8, BLOCK), F32),
            *arrived, *landed,
            sem((pieces,)), sem((stages * pieces + 2 * stages,)),
            sem((stages * pieces + 2 * stages,)),
        ],
        compiler_params=pltpu.CompilerParams(
            collective_id=0, has_side_effects=True, vmem_limit_bytes=60 * 2**20),
        name="exchange",
    )(held, owners)


def stage_bits(tm, grp):
    grp_bits = list(range(grp.bit_length() - 1))
    base = len(grp_bits)
    tm_bits = list(range(base, base + tm.bit_length() - 1))
    core, rest = tm_bits[:1], tm_bits[1:]
    near, far = rest[: len(rest) // 2], rest[len(rest) // 2 :]
    return core + near + far + grp_bits, core + far + near + grp_bits


def pack(value, bits):
    packed = jnp.zeros_like(value)
    for bit in bits:
        packed = packed * 2 + (value >> bit & 1)
    return packed


def swap_halo(series, half):
    axes = ("tm", "grp")
    count = lax.axis_size(axes)
    forward = [(i, i + 1) for i in range(count - 1)]
    backward = [(i + 1, i) for i in range(count - 1)]
    low = lax.ppermute(series[-half:], axes, forward)
    high = lax.ppermute(series[:half], axes, backward)
    return low, high


def bit_parity(value, bits):
    parity = jnp.zeros_like(value)
    for bit in range(bits):
        parity = parity ^ (value >> bit & 1)
    return parity


CHUNKS = 2


def on_device(series, filter_taps, sign_flips, samples):
    rows_dev, columns = series.shape
    half = (filter_taps.shape[0] - 1) // 2
    tm, grp = lax.axis_size("tm"), lax.axis_size("grp")
    devices = tm * grp
    sample_count = samples.shape[0]
    per_device = rows_dev // devices
    copies = sample_count // rows_dev
    me = lax.axis_index("tm") * grp + lax.axis_index("grp")
    even, odd = stage_bits(tm, grp)
    core = even[0]

    relative = jnp.arange(devices, dtype=jnp.int32) ^ me
    other = relative >> core & 1
    as_even = (me >> core & 1) ^ other == 0
    perm = jnp.where(as_even, pack(relative, even), pack(relative, odd))
    order = min(256, rows_dev)
    signs = sign_flips.astype(F32).reshape(rows_dev // order, order)
    low, high = swap_halo(series, half)

    slot = jnp.arange(devices, dtype=jnp.int32)
    hit = perm[None, :] == slot[:, None]
    owner = (samples // rows_dev).astype(F32).reshape(devices, per_device * copies)
    owner = lax.dot_general(hit.astype(F32), owner, (((1,), (0,)), ((), ())),
                            precision=lax.Precision.HIGHEST).astype(jnp.int32)
    owner = owner[: devices // 2].reshape(devices // 2, per_device, copies).transpose(0, 2, 1)
    is_even = (me >> core & 1) == 0
    code = jnp.zeros_like(owner)
    for stage, (even_bit, odd_bit) in enumerate(zip(even, odd)):
        code = code + ((owner >> jnp.where(is_even, even_bit, odd_bit) & 1) << stage)
    code = code + (bit_parity(owner & me, devices.bit_length()) << len(even))
    codes = jnp.broadcast_to(code[..., None], code.shape + (BLOCK,))
    held = mixed(devices, perm, filter_taps, series, low, high, signs)
    scale = (rows_dev * devices) ** -0.5
    sums, packed = exchange(tm, grp, scale, held, codes)
    sketch = sums.transpose(1, 0, 2).reshape(-1, columns)
    return sketch, factor(packed, columns, sample_count)


def solution(mesh):
    return jax.shard_map(
        on_device,
        mesh=mesh,
        in_specs=(P(("tm", "grp"), None), P(), P(("tm", "grp")), P()),
        out_specs=(P(("tm", "grp"), None), P()),
        check_vma=False,
    )
```

```python
import functools

import jax
import jax.numpy as jnp
from jax import lax
from jax.experimental import pallas as pl
from jax.experimental.pallas import tpu as pltpu
from jax.sharding import PartitionSpec as P

F32 = jnp.float32
BF16 = jnp.bfloat16


def halves(x):
    high = x.astype(BF16)
    return high, (x - high.astype(F32)).astype(BF16)


def factor_kernel(block, scale, g_ref, r_ref, m_ref, a_ref):
    size = a_ref.shape[0]
    hi = lax.Precision.HIGHEST
    a_ref[...] = jnp.zeros_like(a_ref)
    for q, (i, j) in enumerate(upper_blocks(size // block)):
        depth = block // 8
        part = g_ref[q * depth : (q + 1) * depth].reshape(block, block)
        a_ref[i * block : (i + 1) * block, j * block : (j + 1) * block] = part * scale
    tiles_count = block // 8
    eye_row = lax.broadcasted_iota(jnp.int32, (8, block), 0)
    eye_col = lax.broadcasted_iota(jnp.int32, (8, block), 1)
    step = 4

    def lane(value, k):
        return jnp.broadcast_to(value[:, k : k + 1], (8, block))

    def panel(p, carry):
        at = pl.multiple_of(p * block, block)
        left, right = [], []
        for t in range(tiles_count):
            left.append(a_ref[pl.ds(pl.multiple_of(at + 8 * t, 8), 8), pl.ds(at, block)])
            right.append((eye_row + 8 * t == eye_col).astype(F32))
        for k in range(0, block, step):
            home, top = divmod(k, 8)
            spread = lambda v, r: jnp.broadcast_to(v[r : r + 1, :], (8, block))
            rows_l = [spread(left[home], top + j) for j in range(step)]
            rows_r = [spread(right[home], top + j) for j in range(step)]
            corner = {(i, j): lane(rows_l[i], k + j) for i in range(step) for j in range(i, step)}
            inverse, link = [], {}
            for j in range(step):
                inverse.append(lax.rsqrt(corner[j, j]))
                for i in range(j + 1, step):
                    link[j, i] = corner[j, i] * inverse[j]
                for i in range(j + 1, step):
                    for h in range(i, step):
                        corner[i, h] = corner[i, h] - link[j, i] * link[j, h]

            def solve(values):
                done = []
                for j in range(step):
                    value = values[j]
                    for i in range(j):
                        value = value - link[i, j] * done[i]
                    done.append(value * inverse[j])
                return done

            rows_l, rows_r = solve(rows_l), solve(rows_r)
            for j in range(step):
                m_ref[k + j : k + j + 1, :] = rows_r[j][0:1, :]
            first = home if top + step < 8 else home + 1
            for t in range(first, tiles_count):
                columns = solve([lane(left[t], k + j) for j in range(step)])
                for j in range(step):
                    column = columns[j]
                    if t == home:
                        column = jnp.where(eye_row >= top + step, column, 0.0)
                    left[t] = left[t] - column * rows_l[j]
                    right[t] = right[t] - column * rows_r[j]
        rows = lax.dot_general(
            m_ref[...], a_ref[pl.ds(at, block), :], (((1,), (0,)), ((), ())),
            precision=hi, preferred_element_type=F32,
        )
        keep = lax.broadcasted_iota(jnp.int32, rows.shape, 1) >= (
            lax.broadcasted_iota(jnp.int32, rows.shape, 0) + at
        )
        rows = jnp.where(keep, rows, 0.0)
        r_ref[pl.ds(at, block), :] = rows

        @pl.when(p < size // block - 1)
        def _():
            a_ref[...] -= lax.dot_general(
                rows, rows, (((0,), (0,)), ((), ())),
                precision=hi, preferred_element_type=F32,
            )
        return carry

    lax.fori_loop(0, size // block, panel, 0)


BLOCK = 128


def upper_blocks(count):
    return [(i, j) for i in range(count) for j in range(i, count)]


def factor(packed, size, sample_count):
    return pl.pallas_call(
        functools.partial(factor_kernel, BLOCK, 1.0 / sample_count),
        out_shape=jax.ShapeDtypeStruct((size, size), F32),
        in_specs=[pl.BlockSpec(memory_space=pltpu.VMEM)],
        out_specs=pl.BlockSpec(memory_space=pltpu.VMEM),
        scratch_shapes=[pltpu.VMEM((BLOCK, BLOCK), F32), pltpu.VMEM((size, size), F32)],
        name="factor",
    )(packed)


PIECES = 4
FIR = 128


def sketch_kernel(tm, grp, scale, copies_of, taps_ref, series_ref, flips_ref, owner_ref,
                  sk_ref, gram_ref, x_ref, halo, x_high, x_low, t_high, t_low, h_ref, y_ref,
                  held, sums, part, *scratch):
    tm_bits, grp_bits = tm.bit_length() - 1, grp.bit_length() - 1
    stages = tm_bits + grp_bits
    devices = tm * grp
    groups = gram_groups(tm_bits, grp_bits)
    arrived, landed = scratch[:PIECES * stages], scratch[PIECES * stages : -3]
    local_sem, send_sem, recv_sem = scratch[-3:]
    t, g = lax.axis_index("tm"), lax.axis_index("grp")
    core = t % 2
    rows, width = x_ref.shape[1], x_ref.shape[2]
    half = halo.shape[1]
    per_device = held.shape[2]
    tap_count = taps_ref.shape[0]
    order = h_ref.shape[0]

    even, odd = stage_bits(tm, grp)
    mix = lambda u, v: u * (1 - core) + v * core

    def own_bit(bit):
        return (t // 2 ** (bit - grp_bits)) % 2 if bit >= grp_bits else (g // 2**bit) % 2

    values, deltas = [], []
    for label in range(stages):
        moves = []
        for bit in (even[label], odd[label]):
            value = own_bit(bit)
            if bit >= grp_bits:
                moves.append((value, (1 - 2 * value) * 2 ** (bit - grp_bits), 0))
            else:
                moves.append((value, 0, (1 - 2 * value) * 2**bit))
        if even[label] == odd[label]:
            value, dt, dg = moves[0]
        else:
            value, dt, dg = (mix(u, v) for u, v in zip(*moves))
        values.append(value)
        deltas.append((dt, dg))

    def peer(labels):
        pt, pg = t, g
        for label in labels:
            pt, pg = pt + deltas[label][0], pg + deltas[label][1]
        return pt, pg

    linear = t * grp + g
    after = (linear + 1) % devices
    before = (linear + devices - 1) % devices
    after, before = (after // grp, after % grp), (before // grp, before % grp)
    greeted = [peer([label]) for label in range(stages)]
    greeted += [peer(pair) for pair in groups if len(pair) > 1] + [after, before]
    barrier = pltpu.get_barrier_semaphore()
    mesh_ids = pl.DeviceIdType.MESH

    def load(c):
        return pltpu.make_async_copy(
            series_ref.at[:, pl.ds(c * width, width)], x_ref.at[c % 2], local_sem.at[c % 2])

    load(0).start()
    for who in greeted:
        pl.semaphore_signal(barrier, inc=1, device_id=who, device_id_type=mesh_ids)
    pl.semaphore_wait(barrier, len(greeted))

    def remote(source, target, slot, who):
        return pltpu.make_async_remote_copy(
            src_ref=source, dst_ref=target, send_sem=send_sem.at[slot],
            recv_sem=recv_sem.at[slot], device_id=who, device_id_type=mesh_ids)

    halo_low = remote(series_ref.at[pl.ds(rows - half, half), :], halo.at[0], 0, after)
    halo_high = remote(series_ref.at[pl.ds(0, half), :], halo.at[1], 1, before)
    halo_low.start()
    halo_high.start()

    lag = lax.broadcasted_iota(jnp.int32, t_high.shape, 1) - lax.broadcasted_iota(
        jnp.int32, t_high.shape, 0)
    band = jnp.zeros(t_high.shape, F32)
    for k in range(tap_count):
        band = jnp.where(lag == k, taps_ref[k], band)
    t_high[...], t_low[...] = halves(band)
    parity = lax.broadcasted_iota(jnp.int32, (order, order), 0) & lax.broadcasted_iota(
        jnp.int32, (order, order), 1)
    for shift in (4, 2, 1):
        parity = parity ^ (parity >> shift)
    h_ref[...] = (1 - 2 * (parity & 1)).astype(F32)
    halo_low.wait_recv()
    halo_high.wait_recv()

    order_of = [list(range(stages))] * PIECES
    order_of[0] = [0] + list(range(tm_bits, stages)) + list(range(1, tm_bits))

    def slab_of(d, c):
        bits = odd if (d >> grp_bits) & 1 else even
        slab = 0
        for label in order_of[c]:
            bit = bits[label]
            value = own_bit(bit)
            slab = slab * 2 + ((1 - value) if (d >> bit) & 1 else value)
        return slab

    def dot(u, v):
        return jnp.dot(u, v, preferred_element_type=F32)

    first_rows = (linear > 0).astype(F32)
    last_rows = (linear < devices - 1).astype(F32)
    hadamards = rows // order
    tile = 8

    def produce(c):
        load(c).wait()
        if c + 1 < PIECES:
            load(c + 1).start()
        lanes = slice(c * width, (c + 1) * width)
        x_high[0:half, :], x_low[0:half, :] = halves(halo[0, :, lanes] * first_rows)
        x_high[half + rows :, :], x_low[half + rows :, :] = halves(halo[1, :, lanes] * last_rows)

        def split(i, carry):
            at = pl.multiple_of(i * order, order)
            high, low = halves(x_ref[c % 2, pl.ds(at, order), :])
            to = pl.multiple_of(at + half, half)
            x_high[pl.ds(to, order), :] = high
            x_low[pl.ds(to, order), :] = low
            return carry

        lax.fori_loop(0, hadamards, split, 0)

        def group(a, carry):
            parts = []
            for piece in range(order // FIR):
                at = pl.multiple_of(a * order + piece * FIR, FIR)
                high = x_high[pl.ds(at, FIR + 2 * half), :]
                low = x_low[pl.ds(at, FIR + 2 * half), :]
                parts.append(
                    dot(t_high[...], high) + (dot(t_high[...], low) + dot(t_low[...], high)))
            filtered = jnp.concatenate(parts, axis=0)
            signed = (h_ref[...] * flips_ref[pl.ds(a, 1), :].astype(F32)).astype(BF16)
            high, low = halves(filtered)
            y_ref[a] = dot(signed, high) + dot(signed, low)
            return carry

        lax.fori_loop(0, hadamards, group, 0)
        cut = order // per_device
        for strip in range(cut):
            slabs = [slab_of(a * cut + strip, c) for a in range(hadamards)]

            def butterfly(b, carry):
                row = pl.multiple_of(b * tile, tile)
                parts = [y_ref[a, pl.ds(strip * per_device + row, tile), :]
                         for a in range(hadamards)]
                step = 1
                while step < hadamards:
                    for i in range(hadamards):
                        if not i & step:
                            u, v = parts[i], parts[i + step]
                            parts[i], parts[i + step] = u + v, u - v
                    step *= 2
                for a in range(hadamards):
                    held[c, slabs[a], pl.ds(row, tile), :] = parts[a]
                return carry

            lax.fori_loop(0, per_device // tile, butterfly, 0)

    def owner_slot(s, c):
        slot = 0
        for place, label in enumerate(order_of[c]):
            if label == 0:
                continue
            bit = (s // 2 ** (stages - 1 - place)) % 2
            bit = bit + values[label] - 2 * bit * values[label]
            spots = [2 ** (b - 1 if b >= grp_bits else b) for b in (even[label], odd[label])]
            slot = slot + bit * (spots[0] if spots[0] == spots[1] else mix(*spots))
        return slot

    def sign(slot, k, bit):
        return (1 - 2 * ((owner_ref[slot, k] >> bit) & 1)).astype(F32)

    def combine(c, i):
        source = arrived[c * stages + i]

        def slab(s, carry):
            slot = owner_slot(s, c)
            for k in range(copies_of):
                value = sign(slot, k, order_of[c][i])
                if i == 0:
                    sums[c, s, k] = held[c, s] + value * source[s]
                else:
                    sums[c, s, k] = sums[c, s, k] + value * source[s, k]
            return carry

        lax.fori_loop(0, devices >> (i + 1), slab, 0)

    copies = {}

    def send(c, i):
        count = devices >> (i + 1)
        whole = held if i == 0 else sums
        copies[c, i] = remote(whole.at[c, pl.ds(count, count)], arrived[c * stages + i],
                              2 + c * stages + i, peer([order_of[c][i]]))
        copies[c, i].start()

    def finish(c, i):
        copies[c, i].wait_recv()
        combine(c, i)
        if i + 1 < stages:
            send(c, i + 1)
        else:
            slot = owner_slot(0, c)
            for k in range(copies_of):
                sk_ref[k, :, c * width : (c + 1) * width] = (
                    sums[c, 0, k] * (sign(slot, k, stages) * scale))

    for c in range(PIECES):
        produce(c)
        send(c, 0)
        if c:
            finish(c - 1, 0)
    finish(PIECES - 1, 0)

    def due(c, i):
        return (8 + 6 * i if c else 11 + 10 * i) + 8 * c * (c > 0) + (i if c == 0 else 0)

    later = [(c, i) for c in range(PIECES) for i in range(1, stages)]
    for c, i in sorted(later, key=lambda ci: (due(*ci), ci[1])):
        finish(c, i)

    blocks = sk_ref.shape[2] // BLOCK
    depth = BLOCK // 8
    total = part.shape[0]
    sketch = sk_ref[...].reshape(copies_of * per_device, sk_ref.shape[2])
    q = 0
    for i in range(blocks):
        product = lax.dot_general(
            sketch[:, i * BLOCK : (i + 1) * BLOCK], sketch[:, i * BLOCK :],
            (((0,), (0,)), ((), ())),
            precision=lax.Precision.HIGHEST, preferred_element_type=F32)
        for j in range(blocks - i):
            part[q * depth : (q + 1) * depth] = product[:, j * BLOCK : (j + 1) * BLOCK].reshape(
                depth, 8, BLOCK)
            q += 1
    if q * depth < total:
        part[q * depth :] = jnp.zeros((total - q * depth, 8, BLOCK), F32)

    slot = 2 + PIECES * stages
    offset, size = 0, total
    plan = []
    for n, labels in enumerate(groups):
        ways = 2 ** len(labels)
        size //= ways
        flight = []
        for r in range(1, ways):
            chosen = [label for p, label in enumerate(labels) if (r >> p) & 1]
            seg = 0
            for label in labels:
                value = values[label]
                seg = seg * 2 + ((1 - value) if label in chosen else value)
            copy = remote(part.at[pl.ds(offset + seg * size, size)], landed[n].at[r - 1],
                          slot, peer(chosen))
            slot += 1
            copy.start()
            flight.append(copy)
            plan.append(copy)
        seg = 0
        for label in labels:
            seg = seg * 2 + values[label]
        offset = offset + seg * size
        total_here = part[pl.ds(offset, size)]
        for r, copy in enumerate(flight):
            copy.wait_recv()
            total_here = total_here + landed[n][r]
        target = part if n + 1 < len(groups) else gram_ref
        target[pl.ds(offset, size)] = total_here
    for labels in reversed(groups):
        ways = 2 ** len(labels)
        span = pl.ds(offset, size)
        flight = []
        for r in range(1, ways):
            chosen = [label for p, label in enumerate(labels) if (r >> p) & 1]
            copy = remote(gram_ref.at[span], gram_ref.at[span], slot, peer(chosen))
            slot += 1
            copy.start()
            flight.append(copy)
            plan.append(copy)
        for copy in flight:
            copy.wait_recv()
        seg = 0
        for label in labels:
            seg = seg * 2 + values[label]
        offset = offset - seg * size
        size *= ways
    halo_low.wait_send()
    halo_high.wait_send()
    for copy in list(copies.values()) + plan:
        copy.wait_send()


def gram_groups(tm_bits, grp_bits):
    def pairs(labels):
        return [labels[i : i + 2] for i in range(0, len(labels), 2)]

    return [[0]] + pairs(list(range(1, tm_bits))) + pairs(
        list(range(tm_bits, tm_bits + grp_bits)))


def sketch_and_gram(tm, grp, scale, copies_of, taps, series, flips, owners):
    rows, columns = series.shape
    devices = tm * grp
    half = (taps.shape[0] - 1) // 2
    per_device = rows // devices
    width = columns // PIECES
    order = flips.shape[1]
    stages = devices.bit_length() - 1
    groups = gram_groups(tm.bit_length() - 1, grp.bit_length() - 1)
    blocks = columns // BLOCK
    needed = blocks * (blocks + 1) // 2 * (BLOCK // 8)
    total = -(-needed // devices) * devices
    arrived = []
    for _ in range(PIECES):
        arrived.append(pltpu.VMEM((devices // 2, per_device, width), F32))
        for i in range(1, stages):
            arrived.append(pltpu.VMEM((devices >> (i + 1), copies_of, per_device, width), F32))
    landed, size, hops = [], total, 0
    for labels in groups:
        size >>= len(labels)
        hops += 2 ** len(labels) - 1
        landed.append(pltpu.VMEM((2 ** len(labels) - 1, size, 8, BLOCK), F32))
    slots = 2 + PIECES * stages + 2 * hops
    sem = pltpu.SemaphoreType.DMA
    vmem = pl.BlockSpec(memory_space=pltpu.VMEM)
    return pl.pallas_call(
        functools.partial(sketch_kernel, tm, grp, scale, copies_of),
        out_shape=(jax.ShapeDtypeStruct((copies_of, per_device, columns), F32),
                   jax.ShapeDtypeStruct((total, 8, BLOCK), F32)),
        in_specs=[pl.BlockSpec(memory_space=pltpu.SMEM), pl.BlockSpec(memory_space=pl.ANY),
                  vmem, vmem],
        out_specs=(vmem, vmem),
        scratch_shapes=[
            pltpu.VMEM((2, rows, width), F32),
            pltpu.VMEM((2, half, columns), F32),
            pltpu.VMEM((rows + 2 * half, width), BF16),
            pltpu.VMEM((rows + 2 * half, width), BF16),
            pltpu.VMEM((FIR, FIR + 2 * half), BF16),
            pltpu.VMEM((FIR, FIR + 2 * half), BF16),
            pltpu.VMEM((order, order), F32),
            pltpu.VMEM((rows // order, order, width), F32),
            pltpu.VMEM((PIECES, devices, per_device, width), F32),
            pltpu.VMEM((PIECES, devices // 2, copies_of, per_device, width), F32),
            pltpu.VMEM((total, 8, BLOCK), F32),
            *arrived, *landed, sem((2,)), sem((slots,)), sem((slots,)),
        ],
        compiler_params=pltpu.CompilerParams(
            collective_id=0, has_side_effects=True, vmem_limit_bytes=60 * 2**20),
        name="sketch",
    )(taps, series, flips, owners)


def stage_bits(tm, grp):
    grp_bits = list(range(grp.bit_length() - 1))
    base = len(grp_bits)
    tm_bits = list(range(base, base + tm.bit_length() - 1))
    core, rest = tm_bits[:1], tm_bits[1:]
    near, far = rest[: len(rest) // 2], rest[len(rest) // 2 :]
    return core + near + far + grp_bits, core + far + near + grp_bits


def bit_parity(value, bits):
    parity = jnp.zeros_like(value)
    for bit in range(bits):
        parity = parity ^ (value >> bit & 1)
    return parity


def on_device(series, filter_taps, sign_flips, samples):
    rows_dev, columns = series.shape
    tm, grp = lax.axis_size("tm"), lax.axis_size("grp")
    devices = tm * grp
    sample_count = samples.shape[0]
    per_device = rows_dev // devices
    copies = sample_count // rows_dev
    core = lax.axis_index("tm") % 2
    me = lax.axis_index("tm") * grp + lax.axis_index("grp")
    even, odd = stage_bits(tm, grp)
    order = min(256, rows_dev)

    owner = (samples // rows_dev).reshape(tm // 2, 2, grp, per_device, copies)
    owner = lax.dynamic_index_in_dim(owner, core, 1, keepdims=False)
    owner = owner.reshape(devices // 2, per_device, copies).transpose(0, 2, 1)
    code = jnp.zeros_like(owner)
    for stage, (even_bit, odd_bit) in enumerate(zip(even, odd)):
        code = code + ((owner >> jnp.where(core == 0, even_bit, odd_bit) & 1) << stage)
    code = code + (bit_parity(owner & me, devices.bit_length()) << len(even))
    codes = jnp.broadcast_to(code[..., None], code.shape + (columns // PIECES,))
    sums, packed = sketch_and_gram(
        tm, grp, (rows_dev * devices) ** -0.5, copies, filter_taps, series,
        sign_flips.reshape(rows_dev // order, order), codes)
    sketch = sums.transpose(1, 0, 2).reshape(-1, columns)
    return sketch, factor(packed, columns, sample_count)


def solution(mesh):
    return jax.shard_map(
        on_device,
        mesh=mesh,
        in_specs=(P(("tm", "grp"), None), P(), P(("tm", "grp")), P()),
        out_specs=(P(("tm", "grp"), None), P()),
        check_vma=False,
    )
```

```python
import functools

import jax
import jax.numpy as jnp
from jax import lax
from jax.experimental import pallas as pl
from jax.experimental.pallas import tpu as pltpu
from jax.sharding import PartitionSpec as P

F32 = jnp.float32
BF16 = jnp.bfloat16


def halves(x):
    high = x.astype(BF16)
    return high, (x - high.astype(F32)).astype(BF16)


def factor_kernel(block, scale, g_ref, r_ref, m_ref, a_ref):
    size = a_ref.shape[0]
    hi = lax.Precision.HIGHEST
    a_ref[...] = jnp.zeros_like(a_ref)
    for q, (i, j) in enumerate(upper_blocks(size // block)):
        depth = block // 8
        part = g_ref[q * depth : (q + 1) * depth].reshape(block, block)
        a_ref[i * block : (i + 1) * block, j * block : (j + 1) * block] = part * scale
    tiles_count = block // 8
    eye_row = lax.broadcasted_iota(jnp.int32, (8, block), 0)
    eye_col = lax.broadcasted_iota(jnp.int32, (8, block), 1)
    step = 8

    def lane(value, k):
        return jnp.broadcast_to(value[:, k : k + 1], (8, block))

    def panel(p, carry):
        at = pl.multiple_of(p * block, block)
        left, right = [], []
        for t in range(tiles_count):
            left.append(a_ref[pl.ds(pl.multiple_of(at + 8 * t, 8), 8), pl.ds(at, block)])
            right.append((eye_row + 8 * t == eye_col).astype(F32))
        for k in range(0, block, step):
            home, top = divmod(k, 8)
            spread = lambda v, r: jnp.broadcast_to(v[r : r + 1, :], (8, block))
            rows_l = [spread(left[home], top + j) for j in range(step)]
            rows_r = [spread(right[home], top + j) for j in range(step)]
            corner = {(i, j): lane(rows_l[i], k + j) for i in range(step) for j in range(i, step)}
            inverse, link = [], {}
            for j in range(step):
                inverse.append(lax.rsqrt(corner[j, j]))
                for i in range(j + 1, step):
                    link[j, i] = corner[j, i] * inverse[j]
                for i in range(j + 1, step):
                    for h in range(i, step):
                        corner[i, h] = corner[i, h] - link[j, i] * link[j, h]

            def solve(values):
                done = []
                for j in range(step):
                    value = values[j]
                    for i in range(j):
                        value = value - link[i, j] * done[i]
                    done.append(value * inverse[j])
                return done

            rows_l, rows_r = solve(rows_l), solve(rows_r)
            for j in range(step):
                m_ref[k + j : k + j + 1, :] = rows_r[j][0:1, :]
            first = home if top + step < 8 else home + 1
            for t in range(first, tiles_count):
                columns = solve([lane(left[t], k + j) for j in range(step)])
                for j in range(step):
                    column = columns[j]
                    if t == home:
                        column = jnp.where(eye_row >= top + step, column, 0.0)
                    left[t] = left[t] - column * rows_l[j]
                    right[t] = right[t] - column * rows_r[j]
        rows = lax.dot_general(
            m_ref[...], a_ref[pl.ds(at, block), :], (((1,), (0,)), ((), ())),
            precision=hi, preferred_element_type=F32,
        )
        keep = lax.broadcasted_iota(jnp.int32, rows.shape, 1) >= (
            lax.broadcasted_iota(jnp.int32, rows.shape, 0) + at
        )
        rows = jnp.where(keep, rows, 0.0)
        r_ref[pl.ds(at, block), :] = rows

        @pl.when(p < size // block - 1)
        def _():
            a_ref[...] -= lax.dot_general(
                rows, rows, (((0,), (0,)), ((), ())),
                precision=hi, preferred_element_type=F32,
            )
        return carry

    lax.fori_loop(0, size // block, panel, 0)


BLOCK = 128


def upper_blocks(count):
    return [(i, j) for i in range(count) for j in range(i, count)]


def factor(packed, size, sample_count):
    return pl.pallas_call(
        functools.partial(factor_kernel, BLOCK, 1.0 / sample_count),
        out_shape=jax.ShapeDtypeStruct((size, size), F32),
        in_specs=[pl.BlockSpec(memory_space=pltpu.VMEM)],
        out_specs=pl.BlockSpec(memory_space=pltpu.VMEM),
        scratch_shapes=[pltpu.VMEM((BLOCK, BLOCK), F32), pltpu.VMEM((size, size), F32)],
        name="factor",
    )(packed)


PIECES = 4
PARTS = 2
UNITS = PIECES * PARTS
FIR = 128


def sketch_kernel(tm, grp, scale, copies_of, taps_ref, series_ref, flips_ref, owner_ref,
                  sk_ref, gram_ref, x_ref, halo, x_high, x_low, t_high, t_low, h_ref, y_ref,
                  held, sums, part, *scratch):
    tm_bits, grp_bits = tm.bit_length() - 1, grp.bit_length() - 1
    stages = tm_bits + grp_bits
    devices = tm * grp
    groups = gram_groups(tm_bits, grp_bits)
    arrived, landed = scratch[:UNITS * stages], scratch[UNITS * stages : -3]
    local_sem, send_sem, recv_sem = scratch[-3:]
    t, g = lax.axis_index("tm"), lax.axis_index("grp")
    core = t % 2
    rows, width = x_ref.shape[1], x_ref.shape[2]
    half = halo.shape[1]
    per_device = held.shape[2]
    tap_count = taps_ref.shape[0]
    order = h_ref.shape[0]

    even, odd = stage_bits(tm, grp)
    mix = lambda u, v: u * (1 - core) + v * core

    def own_bit(bit):
        return (t // 2 ** (bit - grp_bits)) % 2 if bit >= grp_bits else (g // 2**bit) % 2

    values, deltas = [], []
    for label in range(stages):
        moves = []
        for bit in (even[label], odd[label]):
            value = own_bit(bit)
            if bit >= grp_bits:
                moves.append((value, (1 - 2 * value) * 2 ** (bit - grp_bits), 0))
            else:
                moves.append((value, 0, (1 - 2 * value) * 2**bit))
        if even[label] == odd[label]:
            value, dt, dg = moves[0]
        else:
            value, dt, dg = (mix(u, v) for u, v in zip(*moves))
        values.append(value)
        deltas.append((dt, dg))

    def peer(labels):
        pt, pg = t, g
        for label in labels:
            pt, pg = pt + deltas[label][0], pg + deltas[label][1]
        return pt, pg

    linear = t * grp + g
    after = (linear + 1) % devices
    before = (linear + devices - 1) % devices
    after, before = (after // grp, after % grp), (before // grp, before % grp)
    greeted = [peer([label]) for label in range(stages)]
    greeted += [peer(pair) for pair in groups if len(pair) > 1] + [after, before]
    barrier = pltpu.get_barrier_semaphore()
    mesh_ids = pl.DeviceIdType.MESH

    def load(c):
        return pltpu.make_async_copy(
            series_ref.at[:, pl.ds(c * width, width)], x_ref.at[c % 2], local_sem.at[c % 2])

    load(0).start()
    for who in greeted:
        pl.semaphore_signal(barrier, inc=1, device_id=who, device_id_type=mesh_ids)
    pl.semaphore_wait(barrier, len(greeted))

    def remote(source, target, slot, who):
        return pltpu.make_async_remote_copy(
            src_ref=source, dst_ref=target, send_sem=send_sem.at[slot],
            recv_sem=recv_sem.at[slot], device_id=who, device_id_type=mesh_ids)

    halo_low = remote(series_ref.at[pl.ds(rows - half, half), :], halo.at[0], 0, after)
    halo_high = remote(series_ref.at[pl.ds(0, half), :], halo.at[1], 1, before)
    halo_low.start()
    halo_high.start()

    lag = lax.broadcasted_iota(jnp.int32, t_high.shape, 1) - lax.broadcasted_iota(
        jnp.int32, t_high.shape, 0)
    band = jnp.zeros(t_high.shape, F32)
    for k in range(tap_count):
        band = jnp.where(lag == k, taps_ref[k], band)
    t_high[...], t_low[...] = halves(band)
    parity = lax.broadcasted_iota(jnp.int32, (order, order), 0) & lax.broadcasted_iota(
        jnp.int32, (order, order), 1)
    for shift in (4, 2, 1):
        parity = parity ^ (parity >> shift)
    h_ref[...] = (1 - 2 * (parity & 1)).astype(F32)
    halo_low.wait_recv()
    halo_high.wait_recv()

    order_of = [list(range(stages))] * PIECES
    order_of[0] = [0] + list(range(tm_bits, stages)) + list(range(1, tm_bits))

    def slab_of(d, c):
        bits = odd if (d >> grp_bits) & 1 else even
        slab = 0
        for label in order_of[c]:
            bit = bits[label]
            value = own_bit(bit)
            slab = slab * 2 + ((1 - value) if (d >> bit) & 1 else value)
        return slab

    def dot(u, v):
        return jnp.dot(u, v, preferred_element_type=F32)

    first_rows = (linear > 0).astype(F32)
    last_rows = (linear < devices - 1).astype(F32)
    hadamards = rows // order
    tile = 8

    def produce(c):
        load(c).wait()
        if c + 1 < PIECES:
            load(c + 1).start()
        lanes = slice(c * width, (c + 1) * width)
        x_high[0:half, :], x_low[0:half, :] = halves(halo[0, :, lanes] * first_rows)
        x_high[half + rows :, :], x_low[half + rows :, :] = halves(halo[1, :, lanes] * last_rows)

        def split(i, carry):
            at = pl.multiple_of(i * order, order)
            high, low = halves(x_ref[c % 2, pl.ds(at, order), :])
            to = pl.multiple_of(at + half, half)
            x_high[pl.ds(to, order), :] = high
            x_low[pl.ds(to, order), :] = low
            return carry

        lax.fori_loop(0, hadamards, split, 0)

        def group(a, carry):
            parts = []
            for piece in range(order // FIR):
                at = pl.multiple_of(a * order + piece * FIR, FIR)
                high = x_high[pl.ds(at, FIR + 2 * half), :]
                low = x_low[pl.ds(at, FIR + 2 * half), :]
                parts.append(
                    dot(t_high[...], high) + (dot(t_high[...], low) + dot(t_low[...], high)))
            filtered = jnp.concatenate(parts, axis=0)
            signed = (h_ref[...] * flips_ref[pl.ds(a, 1), :].astype(F32)).astype(BF16)
            high, low = halves(filtered)
            y_ref[a] = dot(signed, high) + dot(signed, low)
            return carry

        lax.fori_loop(0, hadamards, group, 0)
        cut = order // per_device
        for strip in range(cut):
            slabs = [slab_of(a * cut + strip, c) for a in range(hadamards)]

            def butterfly(b, carry):
                row = pl.multiple_of(b * tile, tile)
                parts = [y_ref[a, pl.ds(strip * per_device + row, tile), :]
                         for a in range(hadamards)]
                step = 1
                while step < hadamards:
                    for i in range(hadamards):
                        if not i & step:
                            u, v = parts[i], parts[i + step]
                            parts[i], parts[i + step] = u + v, u - v
                    step *= 2
                for a in range(hadamards):
                    held[c, slabs[a], pl.ds(row, tile), :] = parts[a]
                return carry

            lax.fori_loop(0, per_device // tile, butterfly, 0)

    def owner_slot(s, c):
        slot = 0
        for place, label in enumerate(order_of[c]):
            if label == 0:
                continue
            bit = (s // 2 ** (stages - 1 - place)) % 2
            bit = bit + values[label] - 2 * bit * values[label]
            spots = [2 ** (b - 1 if b >= grp_bits else b) for b in (even[label], odd[label])]
            slot = slot + bit * (spots[0] if spots[0] == spots[1] else mix(*spots))
        return slot

    depth_of = per_device // PARTS

    def strip_of(unit):
        at = unit % PARTS * depth_of
        return unit // PARTS, slice(at, at + depth_of)

    def sign(slot, k, span, bit):
        return (1 - 2 * ((owner_ref[slot, k, span] >> bit) & 1)).astype(F32)

    def combine(unit, i):
        c, span = strip_of(unit)
        source = arrived[unit * stages + i]

        def slab(s, carry):
            slot = owner_slot(s, c)
            for k in range(copies_of):
                value = sign(slot, k, span, order_of[c][i])
                if i == 0:
                    sums[unit, s, k] = held[c, s, span] + value * source[s]
                else:
                    sums[unit, s, k] = sums[unit, s, k] + value * source[s, k]
            return carry

        lax.fori_loop(0, devices >> (i + 1), slab, 0)

    copies = {}

    def send(unit, i):
        c, span = strip_of(unit)
        count = devices >> (i + 1)
        if i == 0:
            source = held.at[c, pl.ds(count, count), pl.ds(span.start, depth_of), :]
        else:
            source = sums.at[unit, pl.ds(count, count)]
        copies[unit, i] = remote(source, arrived[unit * stages + i],
                                 2 + unit * stages + i, peer([order_of[c][i]]))
        copies[unit, i].start()

    def finish(unit, i):
        c, span = strip_of(unit)
        copies[unit, i].wait_recv()
        combine(unit, i)
        if i + 1 < stages:
            send(unit, i + 1)
        else:
            slot = owner_slot(0, c)
            for k in range(copies_of):
                sk_ref[k, span, c * width : (c + 1) * width] = (
                    sums[unit, 0, k] * (sign(slot, k, span, stages) * scale))

    for c in range(PIECES):
        produce(c)
        for p in range(PARTS):
            send(c * PARTS + p, 0)
        for p in range(PARTS):
            if c:
                finish((c - 1) * PARTS + p, 0)
    for p in range(PARTS):
        finish((PIECES - 1) * PARTS + p, 0)

    def due(unit, i):
        c, p = unit // PARTS, unit % PARTS / PARTS
        return 8 + 4 * i + 8 * (c + p) if c else 11 + 7 * i + 11 * p

    later = [(u, i) for u in range(UNITS) for i in range(1, stages)]
    for u, i in sorted(later, key=lambda ui: (due(*ui), ui[1])):
        finish(u, i)

    blocks = sk_ref.shape[2] // BLOCK
    depth = BLOCK // 8
    total = part.shape[0]
    sketch = sk_ref[...].reshape(copies_of * per_device, sk_ref.shape[2])
    q = 0
    for i in range(blocks):
        product = lax.dot_general(
            sketch[:, i * BLOCK : (i + 1) * BLOCK], sketch[:, i * BLOCK :],
            (((0,), (0,)), ((), ())),
            precision=lax.Precision.HIGHEST, preferred_element_type=F32)
        for j in range(blocks - i):
            part[q * depth : (q + 1) * depth] = product[:, j * BLOCK : (j + 1) * BLOCK].reshape(
                depth, 8, BLOCK)
            q += 1
    if q * depth < total:
        part[q * depth :] = jnp.zeros((total - q * depth, 8, BLOCK), F32)

    slot = 2 + UNITS * stages
    offset, size = 0, total
    plan = []
    for n, labels in enumerate(groups):
        ways = 2 ** len(labels)
        size //= ways
        flight = []
        for r in range(1, ways):
            chosen = [label for p, label in enumerate(labels) if (r >> p) & 1]
            seg = 0
            for label in labels:
                value = values[label]
                seg = seg * 2 + ((1 - value) if label in chosen else value)
            copy = remote(part.at[pl.ds(offset + seg * size, size)], landed[n].at[r - 1],
                          slot, peer(chosen))
            slot += 1
            copy.start()
            flight.append(copy)
            plan.append(copy)
        seg = 0
        for label in labels:
            seg = seg * 2 + values[label]
        offset = offset + seg * size
        total_here = part[pl.ds(offset, size)]
        for r, copy in enumerate(flight):
            copy.wait_recv()
            total_here = total_here + landed[n][r]
        target = part if n + 1 < len(groups) else gram_ref
        target[pl.ds(offset, size)] = total_here
    for labels in reversed(groups):
        ways = 2 ** len(labels)
        span = pl.ds(offset, size)
        flight = []
        for r in range(1, ways):
            chosen = [label for p, label in enumerate(labels) if (r >> p) & 1]
            copy = remote(gram_ref.at[span], gram_ref.at[span], slot, peer(chosen))
            slot += 1
            copy.start()
            flight.append(copy)
            plan.append(copy)
        for copy in flight:
            copy.wait_recv()
        seg = 0
        for label in labels:
            seg = seg * 2 + values[label]
        offset = offset - seg * size
        size *= ways
    halo_low.wait_send()
    halo_high.wait_send()
    for copy in list(copies.values()) + plan:
        copy.wait_send()


def gram_groups(tm_bits, grp_bits):
    def pairs(labels):
        return [labels[i : i + 2] for i in range(0, len(labels), 2)]

    return [[0]] + pairs(list(range(1, tm_bits))) + pairs(
        list(range(tm_bits, tm_bits + grp_bits)))


def sketch_and_gram(tm, grp, scale, copies_of, taps, series, flips, owners):
    rows, columns = series.shape
    devices = tm * grp
    half = (taps.shape[0] - 1) // 2
    per_device = rows // devices
    width = columns // PIECES
    order = flips.shape[1]
    stages = devices.bit_length() - 1
    groups = gram_groups(tm.bit_length() - 1, grp.bit_length() - 1)
    blocks = columns // BLOCK
    needed = blocks * (blocks + 1) // 2 * (BLOCK // 8)
    total = -(-needed // devices) * devices
    arrived = []
    thin = per_device // PARTS
    for _ in range(UNITS):
        arrived.append(pltpu.VMEM((devices // 2, thin, width), F32))
        for i in range(1, stages):
            arrived.append(pltpu.VMEM((devices >> (i + 1), copies_of, thin, width), F32))
    landed, size, hops = [], total, 0
    for labels in groups:
        size >>= len(labels)
        hops += 2 ** len(labels) - 1
        landed.append(pltpu.VMEM((2 ** len(labels) - 1, size, 8, BLOCK), F32))
    slots = 2 + UNITS * stages + 2 * hops
    sem = pltpu.SemaphoreType.DMA
    vmem = pl.BlockSpec(memory_space=pltpu.VMEM)
    return pl.pallas_call(
        functools.partial(sketch_kernel, tm, grp, scale, copies_of),
        out_shape=(jax.ShapeDtypeStruct((copies_of, per_device, columns), F32),
                   jax.ShapeDtypeStruct((total, 8, BLOCK), F32)),
        in_specs=[pl.BlockSpec(memory_space=pltpu.SMEM), pl.BlockSpec(memory_space=pl.ANY),
                  vmem, vmem],
        out_specs=(vmem, vmem),
        scratch_shapes=[
            pltpu.VMEM((2, rows, width), F32),
            pltpu.VMEM((2, half, columns), F32),
            pltpu.VMEM((rows + 2 * half, width), BF16),
            pltpu.VMEM((rows + 2 * half, width), BF16),
            pltpu.VMEM((FIR, FIR + 2 * half), BF16),
            pltpu.VMEM((FIR, FIR + 2 * half), BF16),
            pltpu.VMEM((order, order), F32),
            pltpu.VMEM((rows // order, order, width), F32),
            pltpu.VMEM((PIECES, devices, per_device, width), F32),
            pltpu.VMEM((UNITS, devices // 2, copies_of, thin, width), F32),
            pltpu.VMEM((total, 8, BLOCK), F32),
            *arrived, *landed, sem((2,)), sem((slots,)), sem((slots,)),
        ],
        compiler_params=pltpu.CompilerParams(
            collective_id=0, has_side_effects=True, vmem_limit_bytes=60 * 2**20),
        name="sketch",
    )(taps, series, flips, owners)


def stage_bits(tm, grp):
    grp_bits = list(range(grp.bit_length() - 1))
    base = len(grp_bits)
    tm_bits = list(range(base, base + tm.bit_length() - 1))
    core, rest = tm_bits[:1], tm_bits[1:]
    near, far = rest[: len(rest) // 2], rest[len(rest) // 2 :]
    return core + near + far + grp_bits, core + far + near + grp_bits


def bit_parity(value, bits):
    parity = jnp.zeros_like(value)
    for bit in range(bits):
        parity = parity ^ (value >> bit & 1)
    return parity


def on_device(series, filter_taps, sign_flips, samples):
    rows_dev, columns = series.shape
    tm, grp = lax.axis_size("tm"), lax.axis_size("grp")
    devices = tm * grp
    sample_count = samples.shape[0]
    per_device = rows_dev // devices
    copies = sample_count // rows_dev
    core = lax.axis_index("tm") % 2
    me = lax.axis_index("tm") * grp + lax.axis_index("grp")
    even, odd = stage_bits(tm, grp)
    order = min(256, rows_dev)

    owner = (samples // rows_dev).reshape(tm // 2, 2, grp, per_device, copies)
    owner = lax.dynamic_index_in_dim(owner, core, 1, keepdims=False)
    owner = owner.reshape(devices // 2, per_device, copies).transpose(0, 2, 1)
    code = jnp.zeros_like(owner)
    for stage, (even_bit, odd_bit) in enumerate(zip(even, odd)):
        code = code + ((owner >> jnp.where(core == 0, even_bit, odd_bit) & 1) << stage)
    code = code + (bit_parity(owner & me, devices.bit_length()) << len(even))
    codes = jnp.broadcast_to(code[..., None], code.shape + (columns // PIECES,))
    sums, packed = sketch_and_gram(
        tm, grp, (rows_dev * devices) ** -0.5, copies, filter_taps, series,
        sign_flips.reshape(rows_dev // order, order), codes)
    sketch = sums.transpose(1, 0, 2).reshape(-1, columns)
    return sketch, factor(packed, columns, sample_count)


def solution(mesh):
    return jax.shard_map(
        on_device,
        mesh=mesh,
        in_specs=(P(("tm", "grp"), None), P(), P(("tm", "grp")), P()),
        out_specs=(P(("tm", "grp"), None), P()),
        check_vma=False,
    )
```
